32 devices in a mesh: row: 2 (over x), col: 4 (over z), depth: 4 (over y, core).
Axes of the slice: x: 2, y: 2, z: 4, core: 2. Of those that a mesh axis runs over, the one named last changes fastest.
Arguments:
- x_blocks: bfloat16 [32, 4, 256, 256], P(('row', 'col'), 'depth'), may hold values from -0.25 to 0.25
- x_columns: int32 [32, 4], P(('row', 'col'), 'depth'), may hold values from 0 to 31, as said below
- h_blocks: bfloat16 [32, 4, 256, 256], P(('row', 'col')), may hold values from -6 to 6
- h_columns: int32 [32, 4], P(('row', 'col')), may hold values from 0 to 31, as said below
- p_columns: int32 [32, 4], P(('row', 'col')), may hold values from 0 to 31, as said below
- q_columns: int32 [32, 4], P(('row', 'col')), may hold values from 0 to 31, as said below
Outputs:
- product_p: bfloat16 [32, 4, 256, 256], P(('row', 'col'), 'depth')
- product_q: bfloat16 [32, 4, 256, 256], P(('row', 'col'), 'depth')
The draws below stay inside these ranges and needn't reach their ends.
Inputs may be any that keep to these rules, and one draw needn't show every extreme that they name: `x_columns`: row i holds 4 distinct block columns (i + o) mod 32 with -2 <= o <= 2. `h_columns`: row i holds 4 distinct block columns (i + o) mod 32 with -2 <= o <= 2. `p_columns`: row i holds 4 distinct block columns (i + o) mod 32 with -4 <= o <= 4. `q_columns`: row i holds 4 distinct block columns (i + o) mod 32 with -6 <= o <= 6.
All inputs are finite; a program needn't handle non-finite values.
Results may differ from the reference program's by a relative error of at most 0.0049.
Values may be sent and summed in bfloat16 or wider, within the bound.
A program may use at most 64 MiB of HBM per device.

```python
import jax
import jax.numpy as jnp
from jax import lax

BLOCK = 256
SLOTS = 4
REACH = 2
PSLOTS = 4
QSLOTS = 4
NBLOCKS = 32


def banded_columns(key, count, spread):
    offsets = jax.vmap(lambda sub_key: jax.random.permutation(sub_key, 2 * spread + 1)[:count])(jax.random.split(key, NBLOCKS))
    rows_index = jnp.arange(NBLOCKS, dtype=jnp.int32)[:, None]
    return jnp.mod(rows_index + offsets.astype(jnp.int32) - spread, NBLOCKS).astype(jnp.int32)


def draw_x_columns(key, part):
    return banded_columns(jax.random.fold_in(key, 11), SLOTS, REACH)


def draw_h_columns(key, part):
    return banded_columns(jax.random.fold_in(key, 22), SLOTS, REACH)


def draw_p_columns(key, part):
    return banded_columns(jax.random.fold_in(key, 33), PSLOTS, 2 * REACH)


def draw_q_columns(key, part):
    return banded_columns(jax.random.fold_in(key, 44), QSLOTS, 3 * REACH)


def block_levels(key, shape, pieces, smallest, largest):
    gain = 1.0
    for axis_at, parts in pieces:
        draws = jax.random.uniform(jax.random.fold_in(jax.random.fold_in(key, 6), axis_at), (parts,), jnp.float32, smallest / len(pieces), largest / len(pieces))
        gain = gain * jnp.repeat(jnp.exp(draws), shape[axis_at] // parts).reshape((-1,) + (1,) * (len(shape) - 1 - axis_at))
    return gain


def centred(own_key, extent, scale, bound, cuts=(), held_as=jnp.bfloat16):
    values = scale * jax.random.normal(own_key, extent, jnp.float32)
    if cuts:
        values = values * block_levels(own_key, extent, cuts, -0.22, 0.18)
    return jnp.clip(values, -bound, bound).astype(held_as)


def setup_inputs(seed: int = 0) -> dict:
    splits = jax.random.split(jax.random.key(seed), 7)
    return {
        "x_blocks": centred(splits[0], (NBLOCKS, SLOTS, BLOCK, BLOCK), (2 * BLOCK) ** -0.5, 0.25, ((0, 8), (1, 4))),
        "x_columns": draw_x_columns(jax.random.fold_in(splits[6], 71), 0),
        "h_blocks": centred(splits[2], (NBLOCKS, SLOTS, BLOCK, BLOCK), 1.0, 6.0, ((0, 8),)),
        "h_columns": draw_h_columns(jax.random.fold_in(splits[6], 71), 0),
        "p_columns": draw_p_columns(jax.random.fold_in(splits[6], 71), 0),
        "q_columns": draw_q_columns(jax.random.fold_in(splits[6], 71), 0),
    }


def sparse_rows(left_blocks, left_columns, wanted, right_blocks, right_columns):
    fetched = right_blocks[left_columns].astype(jnp.float32)
    fetched_columns = right_columns[left_columns]
    chosen_mask = (fetched_columns[:, :, None] == wanted[None, None, :]).astype(jnp.float32)
    chosen = jnp.einsum('kmp,kmbc->kpbc', chosen_mask, fetched, precision=lax.Precision.HIGHEST)
    return jnp.einsum('kab,kpbc->pac', left_blocks.astype(jnp.float32), chosen, precision=lax.Precision.HIGHEST)


def reference(x_blocks, x_columns, h_blocks, h_columns, p_columns, q_columns):
    def first_row(items):
        left_blocks, left_columns, wanted = items
        return sparse_rows(left_blocks, left_columns, wanted, h_blocks, h_columns).astype(jnp.bfloat16)

    product_p = lax.map(first_row, (x_blocks, x_columns, p_columns))

    def second_row(items):
        left_blocks, left_columns, wanted = items
        return sparse_rows(left_blocks, left_columns, wanted, x_blocks, x_columns).astype(jnp.bfloat16)

    product_q = lax.map(second_row, (product_p, p_columns, q_columns))
    return product_p, product_q
```

```python
import functools

import jax
import jax.numpy as jnp
from jax import lax
from jax.experimental import pallas as pl
from jax.experimental.pallas import tpu as pltpu
from jax.sharding import PartitionSpec as P

REACH = 2
MESH = pl.DeviceIdType.MESH


def kernel(
    sizes, x_ref, h_ref, meta_ref, p_cols, q_cols,
    out_p, out_q,
    xb, xo, hb, pb, qb, meta_v, meta_s, send_sem, recv_sem, local_sem,
):
    rows_n, cols_n, rows_here, slots, block = sizes
    groups = rows_n * cols_n
    all_rows = groups * rows_here
    half_w = block // 2
    own_rows = rows_here // 2
    wide = 2 * REACH
    group = lax.axis_index("row") * cols_n + lax.axis_index("col")
    d = lax.axis_index("depth")
    y = d // 2
    c = lax.rem(d, 2)
    first_row = group * rows_here

    def at(step, depth):
        g = lax.rem(group + step + groups, groups)
        return (g // cols_n, lax.rem(g, cols_n), depth)

    def other(dy, dc):
        yy = lax.rem(y + dy, 2)
        cc = lax.rem(c + dc, 2)
        return yy, cc, yy * 2 + cc

    mates = [(0, 1), (1, 0), (1, 1)]
    peers = [(0, dy, dc) for dy, dc in mates]
    peers += [(s, dy, dc) for s in (1, -1) for dy in (0, 1) for dc in (0, 1)]

    barrier = pltpu.get_barrier_semaphore()
    for s, dy, dc in peers:
        pl.semaphore_signal(
            barrier, inc=1, device_id=at(s, other(dy, dc)[2]), device_id_type=MESH
        )
    pl.semaphore_wait(barrier, len(peers))

    counts = {"remote": 0, "local": 0}
    started = []

    def send(src, dst, to):
        n = counts["remote"]
        counts["remote"] = n + 1
        copy = pltpu.make_async_remote_copy(
            src_ref=src, dst_ref=dst, send_sem=send_sem.at[n], recv_sem=recv_sem.at[n],
            device_id=to, device_id_type=MESH,
        )
        copy.start()
        started.append(copy)
        return copy

    def move(src, dst):
        n = counts["local"]
        counts["local"] = n + 1
        copy = pltpu.make_async_copy(src, dst, local_sem.at[n])
        copy.start()
        return copy

    def side(which):
        return pl.ds(pl.multiple_of(which * half_w, half_w), half_w)

    here = pl.ds(wide, rows_here)
    over = at(0, other(1, 0)[2])
    partner = at(0, other(0, 1)[2])

    metas = [
        send(meta_ref, meta_v.at[(1 - s) * slots + d], at(s, other(dy, dc)[2]))
        for s, dy, dc in peers
    ]
    own_meta = move(meta_ref, meta_v.at[slots + d])

    y_near = send(x_ref.at[:, 0, :, side(1 - y)], xb.at[here, c, y], over)
    local_x = move(x_ref.at[:, 0, :, side(y)], xb.at[here, c, y])

    mine = pl.ds(c * (slots // 2), slots // 2)
    h_up = send(
        h_ref.at[pl.ds(rows_here - REACH, REACH), mine, :, side(y)],
        hb.at[pl.ds(0, REACH), mine], at(1, d),
    )
    h_down = send(
        h_ref.at[pl.ds(0, REACH), mine, :, side(y)],
        hb.at[pl.ds(REACH + rows_here, REACH), mine], at(-1, d),
    )
    y_far = send(x_ref.at[:, 0, :, side(y)], xo.at[:, c, y], over)
    local_o = move(x_ref.at[:, 0, :, side(1 - y)], xo.at[:, c, y])
    local_h = move(h_ref.at[:, :, :, side(y)], hb.at[pl.ds(REACH, rows_here)])
    d2d = [
        send(x_ref.at[:, 0, :, side(y)], xb.at[here, c, y], partner),
        send(x_ref.at[:, 0, :, side(1 - y)], xo.at[:, c, y], partner),
    ]
    zeros = jnp.zeros((block, half_w), hb.dtype)
    hb[rows_here + 2 * REACH, 0] = zeros
    xb[rows_here + 2 * wide, 0, 0] = zeros

    local_x.wait()
    y_near.wait_recv()
    rim = []
    for step in range(rows_here):
        down = rows_here - 1 - step
        rim.append((send(xb.at[wide + down, c], xb.at[down, c], at(1, d)), down))
        rim.append(
            (
                send(xb.at[wide + step, c], xb.at[wide + rows_here + step, c], at(-1, d)),
                wide + rows_here + step,
            )
        )
    d2d.append(send(xb.at[here, c, 1 - y], xb.at[here, c, 1 - y], partner))
    y_far.wait_recv()
    d2d.append(send(xo.at[:, c, 1 - y], xo.at[:, c, 1 - y], partner))
    own_meta.wait()
    for copy in metas:
        copy.wait_recv()
    to_smem = move(meta_v, meta_s)
    h_up.wait_recv()
    ref = hb.at[pl.ds(0, REACH), mine]
    d2d.append(send(ref, ref, partner))
    h_down.wait_recv()
    ref = hb.at[pl.ds(REACH + rows_here, REACH), mine]
    d2d.append(send(ref, ref, partner))
    to_smem.wait()
    local_o.wait()
    local_h.wait()
    for copy in d2d:
        copy.wait_recv()

    p_moves = []
    for ii in range(own_rows):
        i = c * own_rows + ii

        def p_block(p, carry, i=i, ii=ii):
            wanted = p_cols[i, p]
            total = jnp.zeros((block, half_w), jnp.float32)
            for k in range(slots):
                column = meta_s[slots + k, i, slots]
                r = lax.rem(column - first_row + REACH + all_rows, all_rows)
                r = jnp.clip(r, 0, rows_here + 2 * REACH - 1)
                part = r + rows_here - REACH
                s = part // rows_here
                row = lax.rem(part, rows_here)
                pick_r = jnp.int32(rows_here + 2 * REACH)
                pick_m = jnp.int32(0)
                for m in range(slots):
                    hit = meta_s[s * slots, row, m] == wanted
                    pick_r = jnp.where(hit, r, pick_r)
                    pick_m = jnp.where(hit, m, pick_m)
                near = xb[wide + i, k % 2, k // 2]
                far = xo[i, k % 2, k // 2]
                left = jnp.concatenate(
                    [jnp.where(y == 0, near, far), jnp.where(y == 0, far, near)], axis=1
                )
                total += jnp.dot(left, hb[pick_r, pick_m], preferred_element_type=jnp.float32)
            pb[y, ii, p] = total.astype(pb.dtype)
            return carry

        lax.fori_loop(0, slots, p_block, 0)
        p_moves.append(send(pb.at[y, ii], pb.at[y, ii], over))

    rim_d2d = []
    for copy, row in rim:
        copy.wait_recv()
        rim_d2d.append(send(xb.at[row, c], xb.at[row, c], partner))
    for copy in p_moves:
        copy.wait_recv()

    where = pl.ds(c * own_rows, own_rows)
    outs = []
    moves = []
    for half in range(2):
        cut = pl.ds(half * half_w, half_w)
        outs.append(
            send(pb.at[half, :, other(0, 1)[2]], out_p.at[where, 0, :, cut], partner)
        )
        moves.append(move(pb.at[half, :, d], out_p.at[where, 0, :, cut]))
    for copy in rim_d2d:
        copy.wait_recv()

    for ii in range(own_rows):
        i = c * own_rows + ii

        def q_block(q, carry, i=i, ii=ii):
            wanted = q_cols[i, q]
            total = jnp.zeros((block, half_w), jnp.float32)
            for p in range(slots):
                r = lax.rem(p_cols[i, p] - first_row + wide + all_rows, all_rows)
                r = jnp.clip(r, 0, rows_here + 2 * wide - 1)
                s = r // rows_here
                row = lax.rem(r, rows_here)
                pick_r = jnp.int32(rows_here + 2 * wide)
                pick_c = jnp.int32(0)
                pick_y = jnp.int32(0)
                for m in range(slots):
                    hit = meta_s[s * slots + m, row, slots] == wanted
                    pick_r = jnp.where(hit, r, pick_r)
                    pick_c = jnp.where(hit, m % 2, pick_c)
                    pick_y = jnp.where(hit, m // 2, pick_y)
                left = jnp.concatenate([pb[0, ii, p], pb[1, ii, p]], axis=1)
                total += jnp.dot(
                    left, xb[pick_r, pick_c, pick_y], preferred_element_type=jnp.float32
                )
            qb[ii, q] = total.astype(qb.dtype)
            return carry

        lax.fori_loop(0, slots, q_block, 0)
        place = pl.ds(c * own_rows + ii, 1)
        for dy, dc in ((1, 0), (1, 1), (0, 1)):
            to = other(dy, dc)[2]
            outs.append(
                send(qb.at[pl.ds(ii, 1), to], out_q.at[place, 0, :, side(y)], at(0, to))
            )
        moves.append(move(qb.at[pl.ds(ii, 1), d], out_q.at[place, 0, :, side(y)]))

    for copy in outs:
        copy.wait_recv()
    for copy in moves:
        copy.wait()
    for copy in started:
        copy.wait_send()


def local(sizes, x_blocks, x_columns, h_blocks, h_columns, p_columns, q_columns):
    rows_n, cols_n = sizes
    rows_here, _, block, _ = x_blocks.shape
    slots = h_blocks.shape[1]
    dtype = x_blocks.dtype
    meta = jnp.concatenate([h_columns, x_columns], axis=1)
    meta = jnp.pad(meta, ((0, 8 - rows_here), (0, 128 - meta.shape[1])))
    half_w = block // 2
    any_space = pl.BlockSpec(memory_space=pl.ANY)
    smem = pl.BlockSpec(memory_space=pltpu.SMEM)
    vmem = pl.BlockSpec(memory_space=pltpu.VMEM)
    out = jax.ShapeDtypeStruct(x_blocks.shape, dtype)
    copies = 64
    return pl.pallas_call(
        functools.partial(kernel, (rows_n, cols_n, rows_here, slots, block)),
        out_shape=(out, out),
        in_specs=[any_space, any_space, vmem, smem, smem],
        out_specs=(any_space, any_space),
        scratch_shapes=[
            pltpu.VMEM((rows_here + 4 * REACH + 1, 2, slots // 2, block, half_w), dtype),
            pltpu.VMEM((rows_here, 2, slots // 2, block, half_w), dtype),
            pltpu.VMEM((rows_here + 2 * REACH + 1, slots, block, half_w), dtype),
            pltpu.VMEM((2, rows_here // 2, slots, block, half_w), dtype),
            pltpu.VMEM((rows_here // 2, slots, block, half_w), dtype),
            pltpu.VMEM((3 * slots, 8, 128), jnp.int32),
            pltpu.SMEM((3 * slots, 8, 128), jnp.int32),
            pltpu.SemaphoreType.DMA((copies,)),
            pltpu.SemaphoreType.DMA((copies,)),
            pltpu.SemaphoreType.DMA((16,)),
        ],
        compiler_params=pltpu.CompilerParams(
            collective_id=0, has_side_effects=True, vmem_limit_bytes=48 * 2**20
        ),
    )(x_blocks, h_blocks, meta, p_columns, q_columns)


def solution(mesh):
    in_specs = (
        P(("row", "col"), "depth", None, None),
        P(("row", "col"), "depth"),
        P(("row", "col"), None, None, None),
        P(("row", "col"), None),
        P(("row", "col"), None),
        P(("row", "col"), None),
    )
    out_specs = (P(("row", "col"), "depth", None, None), P(("row", "col"), "depth", None, None))
    sizes = (mesh.shape["row"], mesh.shape["col"])
    return jax.shard_map(
        functools.partial(local, sizes), mesh=mesh, in_specs=in_specs, out_specs=out_specs,
        check_vma=False,
    )
```

```python
import functools

import jax
import jax.numpy as jnp
from jax import lax
from jax.experimental import pallas as pl
from jax.experimental.pallas import tpu as pltpu
from jax.sharding import PartitionSpec as P

REACH = 2
MESH = pl.DeviceIdType.MESH


def kernel(
    sizes, x_ref, h_ref, xc_ref, hc_ref, pc_ref, qc_ref,
    out_p, out_q,
    xb, xt, xo, hb, pb, qb, qacc, xc_v, hc_v, x_cols, h_cols, p_cols, q_cols,
    send_sem, recv_sem, local_sem,
):
    rows_n, cols_n, rows_here, slots, block = sizes
    groups = rows_n * cols_n
    all_rows = groups * rows_here
    half_w = block // 2
    own_rows = rows_here // 2
    wide = 2 * REACH
    group = lax.axis_index("row") * cols_n + lax.axis_index("col")
    d = lax.axis_index("depth")
    y = d // 2
    c = lax.rem(d, 2)
    first_row = group * rows_here

    def at(step, depth):
        g = lax.rem(group + step + groups, groups)
        return (g // cols_n, lax.rem(g, cols_n), depth)

    def other(dy, dc):
        yy = lax.rem(y + dy, 2)
        cc = lax.rem(c + dc, 2)
        return yy, cc, yy * 2 + cc

    mates = [(0, 1), (1, 0), (1, 1)]
    peers = [(0, dy, dc) for dy, dc in mates]
    peers += [(s, dy, dc) for s in (1, -1) for dy in (0, 1) for dc in (0, 1)]

    barrier = pltpu.get_barrier_semaphore()
    for s, dy, dc in peers:
        pl.semaphore_signal(
            barrier, inc=1, device_id=at(s, other(dy, dc)[2]), device_id_type=MESH
        )
    pl.semaphore_wait(barrier, len(peers))

    counts = {"remote": 0, "local": 0}
    started = []

    def send(src, dst, to):
        n = counts["remote"]
        counts["remote"] = n + 1
        copy = pltpu.make_async_remote_copy(
            src_ref=src, dst_ref=dst, send_sem=send_sem.at[n], recv_sem=recv_sem.at[n],
            device_id=to, device_id_type=MESH,
        )
        copy.start()
        started.append(copy)
        return copy

    def move(src, dst):
        n = counts["local"]
        counts["local"] = n + 1
        copy = pltpu.make_async_copy(src, dst, local_sem.at[n])
        copy.start()
        return copy

    def side(which):
        return pl.ds(pl.multiple_of(which * half_w, half_w), half_w)

    here = pl.ds(wide - 1, rows_here)
    xb_zero = rows_here + 2 * wide - 2
    hb_zero = rows_here + 2 * REACH
    over = at(0, other(1, 0)[2])
    partner = at(0, other(0, 1)[2])

    metas = [
        send(xc_ref, xc_v.at[(1 - s) * slots + d], at(s, other(dy, dc)[2]))
        for s, dy, dc in peers
    ]
    metas += [send(hc_ref, hc_v.at[1 - s], at(s, d)) for s in (1, -1)]
    own_meta = [
        move(xc_ref, xc_v.at[slots + d]), move(hc_ref, hc_v.at[1]),
        move(pc_ref, p_cols), move(qc_ref, q_cols),
    ]

    y_near = send(x_ref.at[:, 0, :, side(1 - y)], xb.at[here, c, y], over)
    local_x = move(x_ref.at[:, 0, :, side(y)], xb.at[here, c, y])

    mine = pl.ds(c * (slots // 2), slots // 2)
    h_up = send(
        h_ref.at[pl.ds(rows_here - REACH, REACH), mine, :, side(y)],
        hb.at[pl.ds(0, REACH), mine], at(1, d),
    )
    h_down = send(
        h_ref.at[pl.ds(0, REACH), mine, :, side(y)],
        hb.at[pl.ds(REACH + rows_here, REACH), mine], at(-1, d),
    )
    y_far = send(x_ref.at[:, 0, :, side(y)], xo.at[:, c, y], over)
    local_o = move(x_ref.at[:, 0, :, side(1 - y)], xo.at[:, c, y])
    local_h = move(h_ref.at[:, :, :, side(y)], hb.at[pl.ds(REACH, rows_here)])
    d2d = [
        send(x_ref.at[:, 0, :, side(y)], xb.at[here, c, y], partner),
        send(x_ref.at[:, 0, :, side(1 - y)], xo.at[:, c, y], partner),
    ]
    zeros = jnp.zeros((block, half_w), hb.dtype)
    hb[hb_zero, 0] = zeros
    xb[xb_zero, 0, 0] = zeros
    xt[3, 0] = zeros

    local_x.wait()
    y_near.wait_recv()
    rim = []
    for step in range(rows_here - 1):
        down = rows_here - 1 - step
        for row, place, to in (
            (down, down, 1), (step, wide + rows_here + step, -1)
        ):
            rim.append((send(xb.at[wide - 1 + row, c], xb.at[place - 1, c], at(to, d)), place - 1))
    late = [
        send(xb.at[wide - 1, c], xt.at[2 * c], at(1, d)),
        send(xb.at[wide - 1 + rows_here - 1, c], xt.at[2 - c], at(-1, d)),
    ]
    d2d.append(send(xb.at[here, c, 1 - y], xb.at[here, c, 1 - y], partner))
    y_far.wait_recv()
    d2d.append(send(xo.at[:, c, 1 - y], xo.at[:, c, 1 - y], partner))
    for copy in own_meta:
        copy.wait()
    for copy in metas:
        copy.wait_recv()
    to_smem = [move(xc_v, x_cols), move(hc_v, h_cols)]
    h_up.wait_recv()
    ref = hb.at[pl.ds(0, REACH), mine]
    d2d.append(send(ref, ref, partner))
    h_down.wait_recv()
    ref = hb.at[pl.ds(REACH + rows_here, REACH), mine]
    d2d.append(send(ref, ref, partner))
    for copy in to_smem:
        copy.wait()
    local_o.wait()
    local_h.wait()
    for copy in d2d:
        copy.wait_recv()

    p_moves = []
    for ii in range(own_rows):
        i = c * own_rows + ii

        def p_block(p, carry, i=i, ii=ii):
            wanted = p_cols[i, p]
            total = jnp.zeros((block, half_w), jnp.float32)
            for k in range(slots):
                column = x_cols[slots + k, 0, i]
                r = lax.rem(column - first_row + REACH + all_rows, all_rows)
                r = jnp.clip(r, 0, rows_here + 2 * REACH - 1)
                part = r + rows_here - REACH
                s = part // rows_here
                row = lax.rem(part, rows_here)
                pick_r = jnp.int32(hb_zero)
                pick_m = jnp.int32(0)
                for m in range(slots):
                    hit = h_cols[s, row, m] == wanted
                    pick_r = jnp.where(hit, r, pick_r)
                    pick_m = jnp.where(hit, m, pick_m)
                near = xb[wide - 1 + i, k % 2, k // 2]
                far = xo[i, k % 2, k // 2]
                left = jnp.concatenate(
                    [jnp.where(y == 0, near, far), jnp.where(y == 0, far, near)], axis=1
                )
                total += jnp.dot(left, hb[pick_r, pick_m], preferred_element_type=jnp.float32)
            pb[y, ii, p] = total.astype(pb.dtype)
            return carry

        lax.fori_loop(0, slots, p_block, 0)
        p_moves.append(send(pb.at[y, ii], pb.at[y, ii], over))

    rim_d2d = []
    for copy, row in rim:
        copy.wait_recv()
        rim_d2d.append(send(xb.at[row, c], xb.at[row, c], partner))
    for copy in p_moves:
        copy.wait_recv()

    where = pl.ds(c * own_rows, own_rows)
    outs = []
    moves = []
    for half in range(2):
        cut = pl.ds(half * half_w, half_w)
        outs.append(
            send(pb.at[half, :, other(0, 1)[2]], out_p.at[where, 0, :, cut], partner)
        )
        moves.append(move(pb.at[half, :, d], out_p.at[where, 0, :, cut]))
    for copy in rim_d2d:
        copy.wait_recv()

    def window(i, p):
        r = lax.rem(p_cols[i, p] - first_row + wide + all_rows, all_rows)
        return jnp.clip(r, 0, last_row)

    def hand_on(ii, q):
        place = pl.ds(c * own_rows + ii, 1)
        dst = out_q.at[place, 0, :, side(y)]
        outs.append(send(qb.at[pl.ds(ii, 1), q], dst, at(0, q)))

    def keep(ii):
        place = pl.ds(c * own_rows + ii, 1)
        moves.append(move(qb.at[pl.ds(ii, 1), d], out_q.at[place, 0, :, side(y)]))

    last_row = rows_here + 2 * wide - 1
    order = ((1, 0), (1, 1), (0, 1))
    for turn in range(own_rows):
        ii = (1 - c) * (own_rows - 1 - turn) + c * turn
        i = c * own_rows + ii

        def q_block(q, carry, i=i, ii=ii, turn=turn):
            wanted = q_cols[i, q]
            total = jnp.zeros((block, half_w), jnp.float32)
            for p in range(slots):
                r = window(i, p)
                s = r // rows_here
                row = lax.rem(r, rows_here)
                inner = jnp.logical_and(r > 0, r < last_row)
                pick_r = jnp.int32(xb_zero)
                pick_c = jnp.int32(0)
                pick_y = jnp.int32(0)
                for m in range(slots):
                    hit = jnp.logical_and(inner, x_cols[s * slots + m, 0, row] == wanted)
                    pick_r = jnp.where(hit, r - 1, pick_r)
                    pick_c = jnp.where(hit, m % 2, pick_c)
                    pick_y = jnp.where(hit, m // 2, pick_y)
                left = jnp.concatenate([pb[0, ii, p], pb[1, ii, p]], axis=1)
                total += jnp.dot(
                    left, xb[pick_r, pick_c, pick_y], preferred_element_type=jnp.float32
                )
            if turn < own_rows - 1:
                qb[ii, q] = total.astype(qb.dtype)
            else:
                qacc[q] = total
            return carry

        lax.fori_loop(0, slots, q_block, 0)
        if turn < own_rows - 1:
            for dy, dc in order:
                hand_on(ii, other(dy, dc)[2])
            keep(ii)

    final = c * last_row
    pick_p = jnp.int32(0)
    some = jnp.int32(0)
    for p in range(slots):
        hit = window(i, p) == final
        pick_p = jnp.where(hit, p, pick_p)
        some = jnp.where(hit, 1, some)
    left = jnp.concatenate([pb[0, ii, pick_p], pb[1, ii, pick_p]], axis=1)
    for copy in late:
        copy.wait_recv()
    last = send(xt.at[2], xt.at[c], partner)
    last.wait_recv()
    for dy, dc in order + ((0, 0),):
        q = other(dy, dc)[2]
        wanted = q_cols[i, q]
        pick_c = jnp.int32(3)
        pick_y = jnp.int32(0)
        for m in range(slots):
            column = x_cols[2 * c * slots + m, 0, c * (rows_here - 1)]
            hit = jnp.logical_and(some == 1, column == wanted)
            pick_c = jnp.where(hit, m % 2, pick_c)
            pick_y = jnp.where(hit, m // 2, pick_y)
        total = qacc[q] + jnp.dot(left, xt[pick_c, pick_y], preferred_element_type=jnp.float32)
        qb[ii, q] = total.astype(qb.dtype)
        if (dy, dc) != (0, 0):
            hand_on(ii, q)
    keep(ii)

    for copy in outs:
        copy.wait_recv()
    for copy in moves:
        copy.wait()
    for copy in started:
        copy.wait_send()


def local(sizes, x_blocks, x_columns, h_blocks, h_columns, p_columns, q_columns):
    rows_n, cols_n = sizes
    rows_here, _, block, _ = x_blocks.shape
    slots = h_blocks.shape[1]
    dtype = x_blocks.dtype
    half_w = block // 2
    any_space = pl.BlockSpec(memory_space=pl.ANY)
    hbm = pl.BlockSpec(memory_space=pltpu.HBM)
    out = jax.ShapeDtypeStruct(x_blocks.shape, dtype)
    copies = 64
    return pl.pallas_call(
        functools.partial(kernel, (rows_n, cols_n, rows_here, slots, block)),
        out_shape=(out, out),
        in_specs=[hbm] * 6,
        out_specs=(any_space, any_space),
        scratch_shapes=[
            pltpu.VMEM((rows_here + 4 * REACH - 1, 2, slots // 2, block, half_w), dtype),
            pltpu.VMEM((4, slots // 2, block, half_w), dtype),
            pltpu.VMEM((rows_here, 2, slots // 2, block, half_w), dtype),
            pltpu.VMEM((rows_here + 2 * REACH + 1, slots, block, half_w), dtype),
            pltpu.VMEM((2, rows_here // 2, slots, block, half_w), dtype),
            pltpu.VMEM((rows_here // 2, slots, block, half_w), dtype),
            pltpu.VMEM((slots, block, half_w), jnp.float32),
            pltpu.VMEM((3 * slots, 1, rows_here), jnp.int32),
            pltpu.VMEM((3,) + h_columns.shape, jnp.int32),
            pltpu.SMEM((3 * slots, 1, rows_here), jnp.int32),
            pltpu.SMEM((3,) + h_columns.shape, jnp.int32),
            pltpu.SMEM(p_columns.shape, jnp.int32),
            pltpu.SMEM(q_columns.shape, jnp.int32),
            pltpu.SemaphoreType.DMA((copies,)),
            pltpu.SemaphoreType.DMA((copies,)),
            pltpu.SemaphoreType.DMA((16,)),
        ],
        compiler_params=pltpu.CompilerParams(
            collective_id=0, has_side_effects=True, vmem_limit_bytes=67043328
        ),
    )(x_blocks, h_blocks, x_columns.T, h_columns, p_columns, q_columns)


def solution(mesh):
    in_specs = (
        P(("row", "col"), "depth", None, None),
        P(("row", "col"), "depth"),
        P(("row", "col"), None, None, None),
        P(("row", "col"), None),
        P(("row", "col"), None),
        P(("row", "col"), None),
    )
    out_specs = (P(("row", "col"), "depth", None, None), P(("row", "col"), "depth", None, None))
    sizes = (mesh.shape["row"], mesh.shape["col"])
    return jax.shard_map(
        functools.partial(local, sizes), mesh=mesh, in_specs=in_specs, out_specs=out_specs,
        check_vma=False,
    )
```

```python
import functools

import jax
import jax.numpy as jnp
from jax import lax
from jax.experimental import pallas as pl
from jax.experimental.pallas import tpu as pltpu
from jax.sharding import PartitionSpec as P

REACH = 2
MESH = pl.DeviceIdType.MESH


def kernel(
    sizes, x_ref, h_ref, xc_ref, hc_ref, pc_ref, qc_ref,
    out_p, out_q,
    xb, xt, xo, hb, pb, qb, qacc, xc_v, hc_v, x_cols, h_cols, p_cols, q_cols,
    send_sem, recv_sem, late_sem, local_sem,
):
    rows_n, cols_n, rows_here, slots, block = sizes
    groups = rows_n * cols_n
    all_rows = groups * rows_here
    half_w = block // 2
    own_rows = rows_here // 2
    wide = 2 * REACH
    group = lax.axis_index("row") * cols_n + lax.axis_index("col")
    d = lax.axis_index("depth")
    y = d // 2
    c = lax.rem(d, 2)
    first_row = group * rows_here

    def at(step, depth):
        g = lax.rem(group + step + groups, groups)
        return (g // cols_n, lax.rem(g, cols_n), depth)

    def other(dy, dc):
        yy = lax.rem(y + dy, 2)
        cc = lax.rem(c + dc, 2)
        return yy, cc, yy * 2 + cc

    mates = [(0, 1), (1, 0), (1, 1)]
    peers = [(0, dy, dc) for dy, dc in mates]
    peers += [(s, dy, dc) for s in (1, -1) for dy in (0, 1) for dc in (0, 1)]

    barrier = pltpu.get_barrier_semaphore()
    for s, dy, dc in peers:
        pl.semaphore_signal(
            barrier, inc=1, device_id=at(s, other(dy, dc)[2]), device_id_type=MESH
        )
    pl.semaphore_wait(barrier, len(peers))

    counts = {"remote": 0, "local": 0}
    started = []

    def send(src, dst, to, landed=None):
        n = counts["remote"]
        counts["remote"] = n + 1
        copy = pltpu.make_async_remote_copy(
            src_ref=src, dst_ref=dst, send_sem=send_sem.at[n],
            recv_sem=recv_sem.at[n] if landed is None else landed,
            device_id=to, device_id_type=MESH,
        )
        copy.start()
        started.append(copy)
        return copy

    def move(src, dst):
        n = counts["local"]
        counts["local"] = n + 1
        copy = pltpu.make_async_copy(src, dst, local_sem.at[n])
        copy.start()
        return copy

    def side(which):
        return pl.ds(pl.multiple_of(which * half_w, half_w), half_w)

    here = pl.ds(wide - 1, rows_here)
    xb_zero = rows_here + 2 * wide - 2
    hb_zero = rows_here + 2 * REACH
    over = at(0, other(1, 0)[2])
    partner = at(0, other(0, 1)[2])

    metas = [
        send(xc_ref, xc_v.at[(1 - s) * slots + d], at(s, other(dy, dc)[2]))
        for s, dy, dc in peers
    ]
    metas += [send(hc_ref, hc_v.at[1 - s], at(s, d)) for s in (1, -1)]
    own_meta = [
        move(xc_ref, xc_v.at[slots + d]), move(hc_ref, hc_v.at[1]),
        move(pc_ref, p_cols), move(qc_ref, q_cols),
    ]

    y_near = send(x_ref.at[:, 0, :, side(1 - y)], xb.at[here, c, y], over)
    local_x = move(x_ref.at[:, 0, :, side(y)], xb.at[here, c, y])

    mine = pl.ds(c * (slots // 2), slots // 2)
    h_up = send(
        h_ref.at[pl.ds(rows_here - REACH, REACH), mine, :, side(y)],
        hb.at[pl.ds(0, REACH), mine], at(1, d),
    )
    h_down = send(
        h_ref.at[pl.ds(0, REACH), mine, :, side(y)],
        hb.at[pl.ds(REACH + rows_here, REACH), mine], at(-1, d),
    )
    y_far = send(x_ref.at[:, 0, :, side(y)], xo.at[:, c, y], over)
    local_o = move(x_ref.at[:, 0, :, side(1 - y)], xo.at[:, c, y])
    local_h = move(h_ref.at[:, :, :, side(y)], hb.at[pl.ds(REACH, rows_here)])
    d2d = [
        send(x_ref.at[:, 0, :, side(y)], xb.at[here, c, y], partner),
        send(x_ref.at[:, 0, :, side(1 - y)], xo.at[:, c, y], partner),
    ]
    zeros = jnp.zeros((block, half_w), hb.dtype)
    hb[hb_zero, 0] = zeros
    xb[xb_zero, 0, 0] = zeros
    xt[2, 0] = zeros

    local_x.wait()
    y_near.wait_recv()
    rim = []
    for step in range(rows_here - 1):
        down = rows_here - 1 - step
        for row, place, to in (
            (down, down, 1), (step, wide + rows_here + step, -1)
        ):
            rim.append((send(xb.at[wide - 1 + row, c], xb.at[place - 1, c], at(to, d)), place - 1))
    late_to = ((wide - 1, at(1, y * 2)), (wide + rows_here - 2, at(-1, y * 2 + 1)))
    for row, to in late_to:
        send(xb.at[row, c], xt.at[c], to, late_sem.at[c])
    late = [
        pltpu.make_async_remote_copy(
            src_ref=xt.at[n], dst_ref=xt.at[n], send_sem=send_sem.at[0], recv_sem=late_sem.at[n],
            device_id=partner, device_id_type=MESH,
        )
        for n in range(2)
    ]
    d2d.append(send(xb.at[here, c, 1 - y], xb.at[here, c, 1 - y], partner))
    y_far.wait_recv()
    d2d.append(send(xo.at[:, c, 1 - y], xo.at[:, c, 1 - y], partner))
    for copy in own_meta:
        copy.wait()
    for copy in metas:
        copy.wait_recv()
    to_smem = [move(xc_v, x_cols), move(hc_v, h_cols)]
    h_up.wait_recv()
    ref = hb.at[pl.ds(0, REACH), mine]
    d2d.append(send(ref, ref, partner))
    h_down.wait_recv()
    ref = hb.at[pl.ds(REACH + rows_here, REACH), mine]
    d2d.append(send(ref, ref, partner))
    for copy in to_smem:
        copy.wait()
    local_o.wait()
    local_h.wait()
    for copy in d2d:
        copy.wait_recv()

    p_moves = []
    for ii in range(own_rows):
        i = c * own_rows + ii

        def p_block(p, carry, i=i, ii=ii):
            wanted = p_cols[i, p]
            total = jnp.zeros((block, half_w), jnp.float32)
            for k in range(slots):
                column = x_cols[slots + k, 0, i]
                r = lax.rem(column - first_row + REACH + all_rows, all_rows)
                r = jnp.clip(r, 0, rows_here + 2 * REACH - 1)
                part = r + rows_here - REACH
                s = part // rows_here
                row = lax.rem(part, rows_here)
                pick_r = jnp.int32(hb_zero)
                pick_m = jnp.int32(0)
                for m in range(slots):
                    hit = h_cols[s, row, m] == wanted
                    pick_r = jnp.where(hit, r, pick_r)
                    pick_m = jnp.where(hit, m, pick_m)
                near = xb[wide - 1 + i, k % 2, k // 2]
                far = xo[i, k % 2, k // 2]
                left = jnp.concatenate(
                    [jnp.where(y == 0, near, far), jnp.where(y == 0, far, near)], axis=1
                )
                total += jnp.dot(left, hb[pick_r, pick_m], preferred_element_type=jnp.float32)
            pb[y, ii, p] = total.astype(pb.dtype)
            return carry

        lax.fori_loop(0, slots, p_block, 0)
        p_moves.append(send(pb.at[y, ii], pb.at[y, ii], over))

    rim_d2d = []
    for copy, row in rim:
        copy.wait_recv()
        rim_d2d.append(send(xb.at[row, c], xb.at[row, c], partner))
    for copy in p_moves:
        copy.wait_recv()

    where = pl.ds(c * own_rows, own_rows)
    outs = []
    moves = []
    for half in range(2):
        cut = pl.ds(half * half_w, half_w)
        outs.append(
            send(pb.at[half, :, other(0, 1)[2]], out_p.at[where, 0, :, cut], partner)
        )
        moves.append(move(pb.at[half, :, d], out_p.at[where, 0, :, cut]))
    for copy in rim_d2d:
        copy.wait_recv()

    def window(i, p):
        r = lax.rem(p_cols[i, p] - first_row + wide + all_rows, all_rows)
        return jnp.clip(r, 0, last_row)

    def hand_on(ii, q):
        place = pl.ds(c * own_rows + ii, 1)
        dst = out_q.at[place, 0, :, side(y)]
        outs.append(send(qb.at[pl.ds(ii, 1), q], dst, at(0, q)))

    def keep(ii):
        place = pl.ds(c * own_rows + ii, 1)
        moves.append(move(qb.at[pl.ds(ii, 1), d], out_q.at[place, 0, :, side(y)]))

    last_row = rows_here + 2 * wide - 1
    order = ((1, 0), (1, 1), (0, 1))
    for turn in range(own_rows):
        ii = (1 - c) * (own_rows - 1 - turn) + c * turn
        i = c * own_rows + ii

        def q_block(q, carry, i=i, ii=ii, turn=turn):
            wanted = q_cols[i, q]
            total = jnp.zeros((block, half_w), jnp.float32)
            for p in range(slots):
                r = window(i, p)
                s = r // rows_here
                row = lax.rem(r, rows_here)
                inner = jnp.logical_and(r > 0, r < last_row)
                pick_r = jnp.int32(xb_zero)
                pick_c = jnp.int32(0)
                pick_y = jnp.int32(0)
                for m in range(slots):
                    hit = jnp.logical_and(inner, x_cols[s * slots + m, 0, row] == wanted)
                    pick_r = jnp.where(hit, r - 1, pick_r)
                    pick_c = jnp.where(hit, m % 2, pick_c)
                    pick_y = jnp.where(hit, m // 2, pick_y)
                left = jnp.concatenate([pb[0, ii, p], pb[1, ii, p]], axis=1)
                total += jnp.dot(
                    left, xb[pick_r, pick_c, pick_y], preferred_element_type=jnp.float32
                )
            if turn < own_rows - 1:
                qb[ii, q] = total.astype(qb.dtype)
            else:
                qacc[q] = total
            return carry

        lax.fori_loop(0, slots, q_block, 0)
        if turn < own_rows - 1:
            for dy, dc in order:
                hand_on(ii, other(dy, dc)[2])
            keep(ii)

    final = c * last_row
    pick_p = jnp.int32(0)
    some = jnp.int32(0)
    for p in range(slots):
        hit = window(i, p) == final
        pick_p = jnp.where(hit, p, pick_p)
        some = jnp.where(hit, 1, some)
    left = jnp.concatenate([pb[0, ii, pick_p], pb[1, ii, pick_p]], axis=1)
    for copy in late:
        copy.wait_recv()
    for dy, dc in order + ((0, 0),):
        q = other(dy, dc)[2]
        wanted = q_cols[i, q]
        pick_c = jnp.int32(2)
        pick_y = jnp.int32(0)
        for m in range(slots):
            column = x_cols[2 * c * slots + m, 0, c * (rows_here - 1)]
            hit = jnp.logical_and(some == 1, column == wanted)
            pick_c = jnp.where(hit, m % 2, pick_c)
            pick_y = jnp.where(hit, m // 2, pick_y)
        total = qacc[q] + jnp.dot(left, xt[pick_c, pick_y], preferred_element_type=jnp.float32)
        qb[ii, q] = total.astype(qb.dtype)
        if (dy, dc) != (0, 0):
            hand_on(ii, q)
    keep(ii)

    for copy in outs:
        copy.wait_recv()
    for copy in moves:
        copy.wait()
    for copy in started:
        copy.wait_send()


def put_out(p_ref, q_ref, p_out, q_out, p_mid, q_mid, sems):
    pieces = p_ref.shape[0]
    ins, outs = [], []
    for n, (src, mid, dst) in enumerate(((p_ref, p_mid, p_out), (q_ref, q_mid, q_out))):
        for i in range(pieces):
            copy = pltpu.make_async_copy(src.at[i], mid.at[i], sems.at[0, n, i])
            copy.start()
            ins.append(copy)
            outs.append(pltpu.make_async_copy(mid.at[i], dst.at[i], sems.at[1, n, i]))
    for copy, out in zip(ins, outs):
        copy.wait()
        out.start()
    for out in outs:
        out.wait()


def local(sizes, x_blocks, x_columns, h_blocks, h_columns, p_columns, q_columns):
    rows_n, cols_n = sizes
    rows_here, _, block, _ = x_blocks.shape
    slots = h_blocks.shape[1]
    dtype = x_blocks.dtype
    half_w = block // 2
    any_space = pl.BlockSpec(memory_space=pl.ANY)
    hbm = pl.BlockSpec(memory_space=pltpu.HBM)
    out = jax.ShapeDtypeStruct(x_blocks.shape, dtype)
    copies = 64
    parts = pl.pallas_call(
        functools.partial(kernel, (rows_n, cols_n, rows_here, slots, block)),
        out_shape=(out, out),
        in_specs=[hbm] * 6,
        out_specs=(hbm, hbm),
        scratch_shapes=[
            pltpu.VMEM((rows_here + 4 * REACH - 1, 2, slots // 2, block, half_w), dtype),
            pltpu.VMEM((3, slots // 2, block, half_w), dtype),
            pltpu.VMEM((rows_here, 2, slots // 2, block, half_w), dtype),
            pltpu.VMEM((rows_here + 2 * REACH + 1, slots, block, half_w), dtype),
            pltpu.VMEM((2, rows_here // 2, slots, block, half_w), dtype),
            pltpu.VMEM((rows_here // 2, slots, block, half_w), dtype),
            pltpu.VMEM((slots, block, half_w), jnp.float32),
            pltpu.VMEM((3 * slots, 1, rows_here), jnp.int32),
            pltpu.VMEM((3,) + h_columns.shape, jnp.int32),
            pltpu.SMEM((3 * slots, 1, rows_here), jnp.int32),
            pltpu.SMEM((3,) + h_columns.shape, jnp.int32),
            pltpu.SMEM(p_columns.shape, jnp.int32),
            pltpu.SMEM(q_columns.shape, jnp.int32),
            pltpu.SemaphoreType.DMA((copies,)),
            pltpu.SemaphoreType.DMA((copies,)),
            pltpu.SemaphoreType.DMA((2,)),
            pltpu.SemaphoreType.DMA((16,)),
        ],
        compiler_params=pltpu.CompilerParams(
            collective_id=0, has_side_effects=True, vmem_limit_bytes=67043328
        ),
    )(x_blocks, h_blocks, x_columns.T, h_columns, p_columns, q_columns)
    return pl.pallas_call(
        put_out,
        out_shape=(out, out),
        in_specs=[hbm] * 2,
        out_specs=(hbm, hbm),
        scratch_shapes=[
            pltpu.VMEM(x_blocks.shape, dtype),
            pltpu.VMEM(x_blocks.shape, dtype),
            pltpu.SemaphoreType.DMA((2, 2, rows_here)),
        ],
        compiler_params=pltpu.CompilerParams(vmem_limit_bytes=67043328),
    )(*parts)


def solution(mesh):
    in_specs = (
        P(("row", "col"), "depth", None, None),
        P(("row", "col"), "depth"),
        P(("row", "col"), None, None, None),
        P(("row", "col"), None),
        P(("row", "col"), None),
        P(("row", "col"), None),
    )
    out_specs = (P(("row", "col"), "depth", None, None), P(("row", "col"), "depth", None, None))
    sizes = (mesh.shape["row"], mesh.shape["col"])
    return jax.shard_map(
        functools.partial(local, sizes), mesh=mesh, in_specs=in_specs, out_specs=out_specs,
        check_vma=False,
    )
```

```python
import functools

import jax
import jax.numpy as jnp
from jax import lax
from jax.experimental import pallas as pl
from jax.experimental.pallas import tpu as pltpu
from jax.sharding import PartitionSpec as P

REACH = 2
MESH = pl.DeviceIdType.MESH


def kernel(
    sizes, x_ref, h_ref, xc_ref, hc_ref, pc_ref, qc_ref,
    out_p, out_q,
    xb, xt, xo, hb, pb, qb, qacc, xc_v, hc_v, x_cols, h_cols, p_cols, q_cols,
    send_sem, recv_sem, late_sem, local_sem,
):
    rows_n, cols_n, rows_here, slots, block = sizes
    groups = rows_n * cols_n
    all_rows = groups * rows_here
    half_w = block // 2
    own_rows = rows_here // 2
    wide = 2 * REACH
    group = lax.axis_index("row") * cols_n + lax.axis_index("col")
    d = lax.axis_index("depth")
    y = d // 2
    c = lax.rem(d, 2)
    first_row = group * rows_here

    def at(step, depth):
        g = lax.rem(group + step + groups, groups)
        return (g // cols_n, lax.rem(g, cols_n), depth)

    def other(dy, dc):
        yy = lax.rem(y + dy, 2)
        cc = lax.rem(c + dc, 2)
        return yy, cc, yy * 2 + cc

    mates = [(0, 1), (1, 0), (1, 1)]
    peers = [(s, dy, dc) for dy in (0, 1) for dc in (0, 1) for s in (1, -1)]
    peers += [(0, dy, dc) for dy, dc in mates]

    barrier = pltpu.get_barrier_semaphore()
    for s, dy, dc in peers:
        pl.semaphore_signal(
            barrier, inc=1, device_id=at(s, other(dy, dc)[2]), device_id_type=MESH
        )

    counts = {"remote": 0, "local": 0}
    started = []

    def send(src, dst, to, landed=None):
        n = counts["remote"]
        counts["remote"] = n + 1
        copy = pltpu.make_async_remote_copy(
            src_ref=src, dst_ref=dst, send_sem=send_sem.at[n],
            recv_sem=recv_sem.at[n] if landed is None else landed,
            device_id=to, device_id_type=MESH,
        )
        copy.start()
        started.append(copy)
        return copy

    def move(src, dst):
        n = counts["local"]
        counts["local"] = n + 1
        copy = pltpu.make_async_copy(src, dst, local_sem.at[n])
        copy.start()
        return copy

    def side(which):
        return pl.ds(pl.multiple_of(which * half_w, half_w), half_w)

    here = pl.ds(wide - 1, rows_here)
    xb_zero = rows_here + 2 * wide - 2
    hb_zero = rows_here + 2 * REACH
    over = at(0, other(1, 0)[2])
    partner = at(0, other(0, 1)[2])

    local_x = move(x_ref.at[:, 0, :, side(y)], xb.at[here, c, y])
    local_o = move(x_ref.at[:, 0, :, side(1 - y)], xo.at[:, c, y])
    local_h = move(h_ref.at[:, :, :, side(y)], hb.at[pl.ds(REACH, rows_here)])
    pl.semaphore_wait(barrier, len(peers))
    mine = pl.ds(c * (slots // 2), slots // 2)
    h_up = send(
        h_ref.at[pl.ds(rows_here - REACH, REACH), mine, :, side(y)],
        hb.at[pl.ds(0, REACH), mine], at(1, d),
    )
    h_down = send(
        h_ref.at[pl.ds(0, REACH), mine, :, side(y)],
        hb.at[pl.ds(REACH + rows_here, REACH), mine], at(-1, d),
    )
    y_near = send(x_ref.at[:, 0, :, side(1 - y)], xb.at[here, c, y], over)

    metas = [
        send(xc_ref, xc_v.at[(1 - s) * slots + d], at(s, other(dy, dc)[2]))
        for s, dy, dc in peers
    ]
    metas += [send(hc_ref, hc_v.at[1 - s], at(s, d)) for s in (1, -1)]
    own_meta = [
        move(xc_ref, xc_v.at[slots + d]), move(hc_ref, hc_v.at[1]),
        move(pc_ref, p_cols), move(qc_ref, q_cols),
    ]

    y_far = send(x_ref.at[:, 0, :, side(y)], xo.at[:, c, y], over)
    d2d = [
        send(x_ref.at[:, 0, :, side(y)], xb.at[here, c, y], partner),
        send(x_ref.at[:, 0, :, side(1 - y)], xo.at[:, c, y], partner),
    ]
    zeros = jnp.zeros((block, half_w), hb.dtype)
    hb[hb_zero, 0] = zeros
    xb[xb_zero, 0, 0] = zeros
    xt[2, 0] = zeros

    local_x.wait()
    y_near.wait_recv()
    rim = []
    for step in range(rows_here - 1):
        down = rows_here - 1 - step
        for row, place, to in (
            (down, down, 1), (step, wide + rows_here + step, -1)
        ):
            rim.append((send(xb.at[wide - 1 + row, c], xb.at[place - 1, c], at(to, d)), place - 1))
    late_to = ((wide - 1, at(1, y * 2)), (wide + rows_here - 2, at(-1, y * 2 + 1)))
    for row, to in late_to:
        send(xb.at[row, c], xt.at[c], to, late_sem.at[c])
    late = [
        pltpu.make_async_remote_copy(
            src_ref=xt.at[n], dst_ref=xt.at[n], send_sem=send_sem.at[0], recv_sem=late_sem.at[n],
            device_id=partner, device_id_type=MESH,
        )
        for n in range(2)
    ]
    d2d.append(send(xb.at[here, c, 1 - y], xb.at[here, c, 1 - y], partner))
    y_far.wait_recv()
    d2d.append(send(xo.at[:, c, 1 - y], xo.at[:, c, 1 - y], partner))
    for copy in own_meta:
        copy.wait()
    for copy in metas:
        copy.wait_recv()
    to_smem = [move(xc_v, x_cols), move(hc_v, h_cols)]
    h_up.wait_recv()
    ref = hb.at[pl.ds(0, REACH), mine]
    d2d.append(send(ref, ref, partner))
    h_down.wait_recv()
    ref = hb.at[pl.ds(REACH + rows_here, REACH), mine]
    d2d.append(send(ref, ref, partner))
    for copy in to_smem:
        copy.wait()
    local_o.wait()
    local_h.wait()
    for copy in d2d:
        copy.wait_recv()

    p_moves = []
    for ii in range(own_rows):
        i = c * own_rows + ii

        def p_block(p, carry, i=i, ii=ii):
            wanted = p_cols[i, p]
            total = jnp.zeros((block, half_w), jnp.float32)
            for k in range(slots):
                column = x_cols[slots + k, 0, i]
                r = lax.rem(column - first_row + REACH + all_rows, all_rows)
                r = jnp.clip(r, 0, rows_here + 2 * REACH - 1)
                part = r + rows_here - REACH
                s = part // rows_here
                row = lax.rem(part, rows_here)
                pick_r = jnp.int32(hb_zero)
                pick_m = jnp.int32(0)
                for m in range(slots):
                    hit = h_cols[s, row, m] == wanted
                    pick_r = jnp.where(hit, r, pick_r)
                    pick_m = jnp.where(hit, m, pick_m)
                near = xb[wide - 1 + i, k % 2, k // 2]
                far = xo[i, k % 2, k // 2]
                left = jnp.concatenate(
                    [jnp.where(y == 0, near, far), jnp.where(y == 0, far, near)], axis=1
                )
                total += jnp.dot(left, hb[pick_r, pick_m], preferred_element_type=jnp.float32)
            pb[y, ii, p] = total.astype(pb.dtype)
            return carry

        lax.fori_loop(0, slots, p_block, 0)
        p_moves.append(send(pb.at[y, ii], pb.at[y, ii], over))

    rim_d2d = []
    for copy, row in rim:
        copy.wait_recv()
        rim_d2d.append(send(xb.at[row, c], xb.at[row, c], partner))
    for copy in p_moves:
        copy.wait_recv()

    where = pl.ds(c * own_rows, own_rows)
    outs = []
    moves = []
    for half in range(2):
        cut = pl.ds(half * half_w, half_w)
        outs.append(
            send(pb.at[half, :, other(0, 1)[2]], out_p.at[where, 0, :, cut], partner)
        )
        moves.append(move(pb.at[half, :, d], out_p.at[where, 0, :, cut]))
    for copy in rim_d2d:
        copy.wait_recv()

    def window(i, p):
        r = lax.rem(p_cols[i, p] - first_row + wide + all_rows, all_rows)
        return jnp.clip(r, 0, last_row)

    def hand_on(ii, q):
        place = pl.ds(c * own_rows + ii, 1)
        dst = out_q.at[place, 0, :, side(y)]
        outs.append(send(qb.at[pl.ds(ii, 1), q], dst, at(0, q)))

    def keep(ii):
        place = pl.ds(c * own_rows + ii, 1)
        moves.append(move(qb.at[pl.ds(ii, 1), d], out_q.at[place, 0, :, side(y)]))

    last_row = rows_here + 2 * wide - 1
    order = ((1, 0), (1, 1), (0, 1))
    for turn in range(own_rows):
        ii = (1 - c) * (own_rows - 1 - turn) + c * turn
        i = c * own_rows + ii

        def q_block(q, carry, i=i, ii=ii, turn=turn):
            wanted = q_cols[i, q]
            total = jnp.zeros((block, half_w), jnp.float32)
            for p in range(slots):
                r = window(i, p)
                s = r // rows_here
                row = lax.rem(r, rows_here)
                inner = jnp.logical_and(r > 0, r < last_row)
                pick_r = jnp.int32(xb_zero)
                pick_c = jnp.int32(0)
                pick_y = jnp.int32(0)
                for m in range(slots):
                    hit = jnp.logical_and(inner, x_cols[s * slots + m, 0, row] == wanted)
                    pick_r = jnp.where(hit, r - 1, pick_r)
                    pick_c = jnp.where(hit, m % 2, pick_c)
                    pick_y = jnp.where(hit, m // 2, pick_y)
                left = jnp.concatenate([pb[0, ii, p], pb[1, ii, p]], axis=1)
                total += jnp.dot(
                    left, xb[pick_r, pick_c, pick_y], preferred_element_type=jnp.float32
                )
            if turn < own_rows - 1:
                qb[ii, q] = total.astype(qb.dtype)
            else:
                qacc[q] = total
            return carry

        lax.fori_loop(0, slots, q_block, 0)
        if turn < own_rows - 1:
            for dy, dc in order:
                hand_on(ii, other(dy, dc)[2])
            keep(ii)

    final = c * last_row
    pick_p = jnp.int32(0)
    some = jnp.int32(0)
    for p in range(slots):
        hit = window(i, p) == final
        pick_p = jnp.where(hit, p, pick_p)
        some = jnp.where(hit, 1, some)
    left = jnp.concatenate([pb[0, ii, pick_p], pb[1, ii, pick_p]], axis=1)
    for copy in late:
        copy.wait_recv()
    for dy, dc in order + ((0, 0),):
        q = other(dy, dc)[2]
        wanted = q_cols[i, q]
        pick_c = jnp.int32(2)
        pick_y = jnp.int32(0)
        for m in range(slots):
            column = x_cols[2 * c * slots + m, 0, c * (rows_here - 1)]
            hit = jnp.logical_and(some == 1, column == wanted)
            pick_c = jnp.where(hit, m % 2, pick_c)
            pick_y = jnp.where(hit, m // 2, pick_y)
        total = qacc[q] + jnp.dot(left, xt[pick_c, pick_y], preferred_element_type=jnp.float32)
        qb[ii, q] = total.astype(qb.dtype)
        if (dy, dc) != (0, 0):
            hand_on(ii, q)
    keep(ii)

    for copy in outs:
        copy.wait_recv()
    for copy in moves:
        copy.wait()
    for copy in started:
        copy.wait_send()


def put_out(p_ref, q_ref, p_out, q_out, p_mid, q_mid, sems):
    pieces = p_ref.shape[0]
    ins, outs = [], []
    for n, (src, mid, dst) in enumerate(((p_ref, p_mid, p_out), (q_ref, q_mid, q_out))):
        for i in range(pieces):
            copy = pltpu.make_async_copy(src.at[i], mid.at[i], sems.at[0, n, i])
            copy.start()
            ins.append(copy)
            outs.append(pltpu.make_async_copy(mid.at[i], dst.at[i], sems.at[1, n, i]))
    for copy, out in zip(ins, outs):
        copy.wait()
        out.start()
    for out in outs:
        out.wait()


def local(sizes, x_blocks, x_columns, h_blocks, h_columns, p_columns, q_columns):
    rows_n, cols_n = sizes
    rows_here, _, block, _ = x_blocks.shape
    slots = h_blocks.shape[1]
    dtype = x_blocks.dtype
    half_w = block // 2
    any_space = pl.BlockSpec(memory_space=pl.ANY)
    hbm = pl.BlockSpec(memory_space=pltpu.HBM)
    out = jax.ShapeDtypeStruct(x_blocks.shape, dtype)
    copies = 64
    parts = pl.pallas_call(
        functools.partial(kernel, (rows_n, cols_n, rows_here, slots, block)),
        out_shape=(out, out),
        in_specs=[hbm] * 6,
        out_specs=(hbm, hbm),
        scratch_shapes=[
            pltpu.VMEM((rows_here + 4 * REACH - 1, 2, slots // 2, block, half_w), dtype),
            pltpu.VMEM((3, slots // 2, block, half_w), dtype),
            pltpu.VMEM((rows_here, 2, slots // 2, block, half_w), dtype),
            pltpu.VMEM((rows_here + 2 * REACH + 1, slots, block, half_w), dtype),
            pltpu.VMEM((2, rows_here // 2, slots, block, half_w), dtype),
            pltpu.VMEM((rows_here // 2, slots, block, half_w), dtype),
            pltpu.VMEM((slots, block, half_w), jnp.float32),
            pltpu.VMEM((3 * slots, 1, rows_here), jnp.int32),
            pltpu.VMEM((3,) + h_columns.shape, jnp.int32),
            pltpu.SMEM((3 * slots, 1, rows_here), jnp.int32),
            pltpu.SMEM((3,) + h_columns.shape, jnp.int32),
            pltpu.SMEM(p_columns.shape, jnp.int32),
            pltpu.SMEM(q_columns.shape, jnp.int32),
            pltpu.SemaphoreType.DMA((copies,)),
            pltpu.SemaphoreType.DMA((copies,)),
            pltpu.SemaphoreType.DMA((2,)),
            pltpu.SemaphoreType.DMA((16,)),
        ],
        compiler_params=pltpu.CompilerParams(
            collective_id=0, has_side_effects=True, vmem_limit_bytes=67043328
        ),
    )(x_blocks, h_blocks, x_columns.T, h_columns, p_columns, q_columns)
    return pl.pallas_call(
        put_out,
        out_shape=(out, out),
        in_specs=[hbm] * 2,
        out_specs=(hbm, hbm),
        scratch_shapes=[
            pltpu.VMEM(x_blocks.shape, dtype),
            pltpu.VMEM(x_blocks.shape, dtype),
            pltpu.SemaphoreType.DMA((2, 2, rows_here)),
        ],
        compiler_params=pltpu.CompilerParams(vmem_limit_bytes=67043328),
    )(*parts)


def solution(mesh):
    in_specs = (
        P(("row", "col"), "depth", None, None),
        P(("row", "col"), "depth"),
        P(("row", "col"), None, None, None),
        P(("row", "col"), None),
        P(("row", "col"), None),
        P(("row", "col"), None),
    )
    out_specs = (P(("row", "col"), "depth", None, None), P(("row", "col"), "depth", None, None))
    sizes = (mesh.shape["row"], mesh.shape["col"])
    return jax.shard_map(
        functools.partial(local, sizes), mesh=mesh, in_specs=in_specs, out_specs=out_specs,
        check_vma=False,
    )
```

```python
import functools

import jax
import jax.numpy as jnp
from jax import lax
from jax.experimental import pallas as pl
from jax.experimental.pallas import tpu as pltpu
from jax.sharding import PartitionSpec as P

REACH = 2
MESH = pl.DeviceIdType.MESH


def kernel(
    sizes, x_ref, h_ref, xc_ref, hc_ref, pc_ref, qc_ref,
    out_p, out_q,
    xb, xt, xo, hb, pb, qb, qacc, xc_v, hc_v, x_cols, h_cols, p_cols, q_cols,
    send_sem, recv_sem, late_sem, local_sem,
):
    rows_n, cols_n, rows_here, slots, block = sizes
    groups = rows_n * cols_n
    all_rows = groups * rows_here
    half_w = block // 2
    own_rows = rows_here // 2
    wide = 2 * REACH
    group = lax.axis_index("row") * cols_n + lax.axis_index("col")
    d = lax.axis_index("depth")
    y = d // 2
    c = lax.rem(d, 2)
    first_row = group * rows_here

    def at(step, depth):
        g = lax.rem(group + step + groups, groups)
        return (g // cols_n, lax.rem(g, cols_n), depth)

    def other(dy, dc):
        yy = lax.rem(y + dy, 2)
        cc = lax.rem(c + dc, 2)
        return yy, cc, yy * 2 + cc

    mates = [(0, 1), (1, 0), (1, 1)]
    peers = [(s, dy, dc) for dy in (0, 1) for dc in (0, 1) for s in (1, -1)]
    peers += [(0, dy, dc) for dy, dc in mates]

    barrier = pltpu.get_barrier_semaphore()
    for s, dy, dc in peers:
        pl.semaphore_signal(
            barrier, inc=1, device_id=at(s, other(dy, dc)[2]), device_id_type=MESH
        )

    counts = {"remote": 0, "local": 0}
    started = []

    def send(src, dst, to, landed=None):
        n = counts["remote"]
        counts["remote"] = n + 1
        copy = pltpu.make_async_remote_copy(
            src_ref=src, dst_ref=dst, send_sem=send_sem.at[n],
            recv_sem=recv_sem.at[n] if landed is None else landed,
            device_id=to, device_id_type=MESH,
        )
        copy.start()
        started.append(copy)
        return copy

    def move(src, dst):
        n = counts["local"]
        counts["local"] = n + 1
        copy = pltpu.make_async_copy(src, dst, local_sem.at[n])
        copy.start()
        return copy

    def side(which):
        return pl.ds(pl.multiple_of(which * half_w, half_w), half_w)

    here = pl.ds(wide - 1, rows_here)
    xb_zero = rows_here + 2 * wide - 2
    hb_zero = rows_here + 2 * REACH
    over = at(0, other(1, 0)[2])
    partner = at(0, other(0, 1)[2])

    local_x = move(x_ref.at[:, 0, :, side(y)], xb.at[here, c, y])
    local_o = move(x_ref.at[:, 0, :, side(1 - y)], xo.at[:, c, y])
    local_h = move(h_ref.at[:, :, :, side(y)], hb.at[pl.ds(REACH, rows_here)])
    pl.semaphore_wait(barrier, len(peers))
    mine = pl.ds(c * (slots // 2), slots // 2)
    h_up = send(
        h_ref.at[pl.ds(rows_here - REACH, REACH), mine, :, side(y)],
        hb.at[pl.ds(0, REACH), mine], at(1, d),
    )
    h_down = send(
        h_ref.at[pl.ds(0, REACH), mine, :, side(y)],
        hb.at[pl.ds(REACH + rows_here, REACH), mine], at(-1, d),
    )
    y_near = send(x_ref.at[:, 0, :, side(1 - y)], xb.at[here, c, y], over)

    metas = [
        send(xc_ref, xc_v.at[(1 - s) * slots + d], at(s, other(dy, dc)[2]))
        for s, dy, dc in peers
    ]
    metas += [send(hc_ref, hc_v.at[1 - s], at(s, d)) for s in (1, -1)]
    own_meta = [
        move(xc_ref, xc_v.at[slots + d]), move(hc_ref, hc_v.at[1]),
        move(pc_ref, p_cols), move(qc_ref, q_cols),
    ]

    y_far = send(x_ref.at[:, 0, :, side(y)], xo.at[:, c, y], over)
    d2d = [
        send(x_ref.at[:, 0, :, side(y)], xb.at[here, c, y], partner),
        send(x_ref.at[:, 0, :, side(1 - y)], xo.at[:, c, y], partner),
    ]
    zeros = jnp.zeros((block, half_w), hb.dtype)
    hb[hb_zero, 0] = zeros
    xb[xb_zero, 0, 0] = zeros
    xt[2, 0] = zeros

    local_x.wait()
    y_near.wait_recv()
    rim = []
    for step in range(rows_here - 1):
        down = rows_here - 1 - step
        for row, place, to in (
            (down, down, 1), (step, wide + rows_here + step, -1)
        ):
            rim.append((send(xb.at[wide - 1 + row, c], xb.at[place - 1, c], at(to, d)), place - 1))
    late_to = ((wide - 1, at(1, y * 2)), (wide + rows_here - 2, at(-1, y * 2 + 1)))
    for row, to in late_to:
        send(xb.at[row, c], xt.at[c], to, late_sem.at[c])
    late = [
        pltpu.make_async_remote_copy(
            src_ref=xt.at[n], dst_ref=xt.at[n], send_sem=send_sem.at[0], recv_sem=late_sem.at[n],
            device_id=partner, device_id_type=MESH,
        )
        for n in range(2)
    ]
    d2d.append(send(xb.at[here, c, 1 - y], xb.at[here, c, 1 - y], partner))
    y_far.wait_recv()
    d2d.append(send(xo.at[:, c, 1 - y], xo.at[:, c, 1 - y], partner))
    for copy in own_meta:
        copy.wait()
    for copy in metas:
        copy.wait_recv()
    to_smem = [move(xc_v, x_cols), move(hc_v, h_cols)]
    h_up.wait_recv()
    ref = hb.at[pl.ds(0, REACH), mine]
    d2d.append(send(ref, ref, partner))
    h_down.wait_recv()
    ref = hb.at[pl.ds(REACH + rows_here, REACH), mine]
    d2d.append(send(ref, ref, partner))
    for copy in to_smem:
        copy.wait()
    local_o.wait()
    local_h.wait()
    for copy in d2d:
        copy.wait_recv()

    p_moves = []
    for ii in range(own_rows):
        i = c * own_rows + ii

        def p_block(p, carry, i=i, ii=ii):
            wanted = p_cols[i, p]
            total = jnp.zeros((block, half_w), jnp.float32)
            for k in range(slots):
                column = x_cols[slots + k, 0, i]
                r = lax.rem(column - first_row + REACH + all_rows, all_rows)
                r = jnp.clip(r, 0, rows_here + 2 * REACH - 1)
                part = r + rows_here - REACH
                s = part // rows_here
                row = lax.rem(part, rows_here)
                pick_r = jnp.int32(hb_zero)
                pick_m = jnp.int32(0)
                for m in range(slots):
                    hit = h_cols[s, row, m] == wanted
                    pick_r = jnp.where(hit, r, pick_r)
                    pick_m = jnp.where(hit, m, pick_m)
                near = xb[wide - 1 + i, k % 2, k // 2]
                far = xo[i, k % 2, k // 2]
                left = jnp.concatenate(
                    [jnp.where(y == 0, near, far), jnp.where(y == 0, far, near)], axis=1
                )
                total += jnp.dot(left, hb[pick_r, pick_m], preferred_element_type=jnp.float32)
            pb[y, ii, p] = total.astype(pb.dtype)
            return carry

        lax.fori_loop(0, slots, p_block, 0)
        p_moves.append(send(pb.at[y, ii], pb.at[y, ii], over))

    rim_d2d = []
    for copy, row in rim:
        copy.wait_recv()
        rim_d2d.append(send(xb.at[row, c], xb.at[row, c], partner))
    for copy in p_moves:
        copy.wait_recv()

    where = pl.ds(c * own_rows, own_rows)
    outs = []
    moves = []
    for half in range(2):
        cut = pl.ds(half * half_w, half_w)
        outs.append(
            send(pb.at[half, :, other(0, 1)[2]], out_p.at[where, 0, :, cut], partner)
        )
        moves.append(move(pb.at[half, :, d], out_p.at[where, 0, :, cut]))
    for copy in rim_d2d:
        copy.wait_recv()

    def window(i, p):
        r = lax.rem(p_cols[i, p] - first_row + wide + all_rows, all_rows)
        return jnp.clip(r, 0, last_row)

    def hand_on(ii, q):
        place = pl.ds(c * own_rows + ii, 1)
        dst = out_q.at[place, 0, :, side(y)]
        outs.append(send(qb.at[pl.ds(ii, 1), q], dst, at(0, q)))

    def keep(ii):
        place = pl.ds(c * own_rows + ii, 1)
        moves.append(move(qb.at[pl.ds(ii, 1), d], out_q.at[place, 0, :, side(y)]))

    last_row = rows_here + 2 * wide - 1
    order = ((1, 0), (1, 1), (0, 1))
    for turn in range(own_rows):
        ii = (1 - c) * (own_rows - 1 - turn) + c * turn
        i = c * own_rows + ii

        def q_block(q, carry, i=i, ii=ii, turn=turn):
            wanted = q_cols[i, q]
            total = jnp.zeros((block, half_w), jnp.float32)
            for p in range(slots):
                r = window(i, p)
                s = r // rows_here
                row = lax.rem(r, rows_here)
                inner = jnp.logical_and(r > 0, r < last_row)
                pick_r = jnp.int32(xb_zero)
                pick_c = jnp.int32(0)
                pick_y = jnp.int32(0)
                for m in range(slots):
                    hit = jnp.logical_and(inner, x_cols[s * slots + m, 0, row] == wanted)
                    pick_r = jnp.where(hit, r - 1, pick_r)
                    pick_c = jnp.where(hit, m % 2, pick_c)
                    pick_y = jnp.where(hit, m // 2, pick_y)
                left = jnp.concatenate([pb[0, ii, p], pb[1, ii, p]], axis=1)
                total += jnp.dot(
                    left, xb[pick_r, pick_c, pick_y], preferred_element_type=jnp.float32
                )
            if turn < own_rows - 1:
                qb[ii, q] = total.astype(qb.dtype)
            else:
                qacc[q] = total
            return carry

        lax.fori_loop(0, slots, q_block, 0)
        if turn < own_rows - 1:
            for dy, dc in order:
                hand_on(ii, other(dy, dc)[2])
            keep(ii)

    final = c * last_row
    pick_p = jnp.int32(0)
    some = jnp.int32(0)
    for p in range(slots):
        hit = window(i, p) == final
        pick_p = jnp.where(hit, p, pick_p)
        some = jnp.where(hit, 1, some)
    left = jnp.concatenate([pb[0, ii, pick_p], pb[1, ii, pick_p]], axis=1)
    for copy in late:
        copy.wait_recv()
    for dy, dc in order + ((0, 0),):
        q = other(dy, dc)[2]
        wanted = q_cols[i, q]
        pick_c = jnp.int32(2)
        pick_y = jnp.int32(0)
        for m in range(slots):
            column = x_cols[2 * c * slots + m, 0, c * (rows_here - 1)]
            hit = jnp.logical_and(some == 1, column == wanted)
            pick_c = jnp.where(hit, m % 2, pick_c)
            pick_y = jnp.where(hit, m // 2, pick_y)
        total = qacc[q] + jnp.dot(left, xt[pick_c, pick_y], preferred_element_type=jnp.float32)
        qb[ii, q] = total.astype(qb.dtype)
        if (dy, dc) != (0, 0):
            hand_on(ii, q)
    keep(ii)

    for copy in outs:
        copy.wait_recv()
    for copy in moves:
        copy.wait()
    for copy in started:
        copy.wait_send()


def put_out(p_ref, q_ref, p_out, q_out, p_mid, q_mid, sems):
    pieces = 2
    span = p_ref.shape[0] // pieces
    at = lambda ref, i: ref.at[pl.ds(i * span, span)]
    ins, outs = [], []
    for n, (src, mid, dst) in enumerate(((p_ref, p_mid, p_out), (q_ref, q_mid, q_out))):
        for i in range(pieces):
            copy = pltpu.make_async_copy(at(src, i), at(mid, i), sems.at[0, n, i])
            copy.start()
            ins.append(copy)
            outs.append(pltpu.make_async_copy(at(mid, i), at(dst, i), sems.at[1, n, i]))
    for copy, out in zip(ins, outs):
        copy.wait()
        out.start()
    for out in outs:
        out.wait()


def local(sizes, x_blocks, x_columns, h_blocks, h_columns, p_columns, q_columns):
    rows_n, cols_n = sizes
    rows_here, _, block, _ = x_blocks.shape
    slots = h_blocks.shape[1]
    dtype = x_blocks.dtype
    half_w = block // 2
    any_space = pl.BlockSpec(memory_space=pl.ANY)
    hbm = pl.BlockSpec(memory_space=pltpu.HBM)
    out = jax.ShapeDtypeStruct(x_blocks.shape, dtype)
    copies = 64
    parts = pl.pallas_call(
        functools.partial(kernel, (rows_n, cols_n, rows_here, slots, block)),
        out_shape=(out, out),
        in_specs=[hbm] * 6,
        out_specs=(hbm, hbm),
        scratch_shapes=[
            pltpu.VMEM((rows_here + 4 * REACH - 1, 2, slots // 2, block, half_w), dtype),
            pltpu.VMEM((3, slots // 2, block, half_w), dtype),
            pltpu.VMEM((rows_here, 2, slots // 2, block, half_w), dtype),
            pltpu.VMEM((rows_here + 2 * REACH + 1, slots, block, half_w), dtype),
            pltpu.VMEM((2, rows_here // 2, slots, block, half_w), dtype),
            pltpu.VMEM((rows_here // 2, slots, block, half_w), dtype),
            pltpu.VMEM((slots, block, half_w), jnp.float32),
            pltpu.VMEM((3 * slots, 1, rows_here), jnp.int32),
            pltpu.VMEM((3,) + h_columns.shape, jnp.int32),
            pltpu.SMEM((3 * slots, 1, rows_here), jnp.int32),
            pltpu.SMEM((3,) + h_columns.shape, jnp.int32),
            pltpu.SMEM(p_columns.shape, jnp.int32),
            pltpu.SMEM(q_columns.shape, jnp.int32),
            pltpu.SemaphoreType.DMA((copies,)),
            pltpu.SemaphoreType.DMA((copies,)),
            pltpu.SemaphoreType.DMA((2,)),
            pltpu.SemaphoreType.DMA((16,)),
        ],
        compiler_params=pltpu.CompilerParams(
            collective_id=0, has_side_effects=True, vmem_limit_bytes=67043328
        ),
    )(x_blocks, h_blocks, x_columns.T, h_columns, p_columns, q_columns)
    return pl.pallas_call(
        put_out,
        out_shape=(out, out),
        in_specs=[hbm] * 2,
        out_specs=(hbm, hbm),
        scratch_shapes=[
            pltpu.VMEM(x_blocks.shape, dtype),
            pltpu.VMEM(x_blocks.shape, dtype),
            pltpu.SemaphoreType.DMA((2, 2, rows_here)),
        ],
        compiler_params=pltpu.CompilerParams(vmem_limit_bytes=67043328),
    )(*parts)


def solution(mesh):
    in_specs = (
        P(("row", "col"), "depth", None, None),
        P(("row", "col"), "depth"),
        P(("row", "col"), None, None, None),
        P(("row", "col"), None),
        P(("row", "col"), None),
        P(("row", "col"), None),
    )
    out_specs = (P(("row", "col"), "depth", None, None), P(("row", "col"), "depth", None, None))
    sizes = (mesh.shape["row"], mesh.shape["col"])
    return jax.shard_map(
        functools.partial(local, sizes), mesh=mesh, in_specs=in_specs, out_specs=out_specs,
        check_vma=False,
    )
```
